512 devices in a mesh: slab: 64 (over z, y), mem: 8 (over x, core).
Axes of the slice: x: 4, y: 4, z: 16, core: 2. Of those that a mesh axis runs over, the one named last changes fastest.
Arguments:
- present_ensemble: float32 [64, 4, 64, 512], P('mem', None, 'slab'), may hold values from -6 to 6
- delayed_ensemble: float32 [64, 2, 4, 64, 512], P('mem', None, None, 'slab'), may hold values from -6 to 6
- spreading_coefficient: float32 [64, 512], P('slab'), may hold values from 0.05 to 0.2
- transport_ratios: float32 [2, 64, 512], P(None, 'slab'), may hold values from -0.3 to 0.3
- obs_value: float32 [2, 256], replicated, may hold values from -6 to 6
- obs_error: float32 [2, 256], replicated, may hold values from 0.4 to 1.2
- obs_noise: float32 [2, 64, 256], replicated, may hold values from -6 to 6
- obs_row: int32 [2, 256], replicated, may hold values from 0 to 63
- obs_col: int32 [2, 256], replicated, may hold values from 1 to 510
- obs_field: int32 [2, 256], replicated, may hold values from 0 to 3
Outputs:
- analysis: float32 [64, 3, 4, 64, 512], P('mem', None, None, 'slab')
The draws below stay inside these ranges and needn't reach their ends.
All inputs are finite; a program needn't handle non-finite values.
Results may differ from the reference program's by a relative error of at most 0.00011.
Values sent between devices are 32-bit elements; how exact they have to be, the bound alone decides.
A program may use at most 64 MiB of HBM per device.

```python
import math
import jax
import jax.numpy as jnp
from jax import lax

NY = 512
FIELDS = 4
MEMBERS = 64
BATCHES = 2
NOBS = 256
NXG = 64


def plant(array, key, low, largest):
    index_at = [jax.random.randint(jax.random.fold_in(key, axis), (), 0, length) for axis, length in enumerate(array.shape)]
    longest = array.shape.index(max(array.shape))
    next_to = index_at[:longest] + [(index_at[longest] + 1) % array.shape[longest]] + index_at[longest + 1:]
    return array.at[tuple(index_at)].set(low).at[tuple(next_to)].set(largest)


def steps_of(own_key, shape, shards, low, top_value):
    gain, own = 1.0, jax.random.fold_in(own_key, 6)
    for axis_at, parts in shards:
        heights = jnp.exp(jax.random.uniform(jax.random.fold_in(own, axis_at), (parts,), jnp.float32, low / len(shards), top_value / len(shards)))
        gain = gain * jnp.repeat(heights, shape[axis_at] // parts).reshape([-1 if axis == axis_at else 1 for axis in range(len(shape))])
    return gain


def scatter_about(stream_key, extent, deviation, most, shards=(), kind=jnp.bfloat16):
    values = deviation * jax.random.normal(stream_key, extent, jnp.float32)
    if shards:
        values = values * steps_of(stream_key, extent, shards, -0.22, 0.18)
    return jnp.clip(values, -most, most).astype(kind)


def setup_inputs(seed: int = 0) -> dict:
    key_list = jax.random.split(jax.random.key(seed), 11)
    return {
        "present_ensemble": scatter_about(key_list[0], (MEMBERS, FIELDS, NXG, NY), 1.0, 6.0, ((0, 8), (2, 64)), jnp.float32),
        "delayed_ensemble": scatter_about(key_list[1], (MEMBERS, 2, FIELDS, NXG, NY), 1.0, 6.0, ((0, 8), (3, 64)), jnp.float32),
        "spreading_coefficient": jnp.clip(jnp.exp(math.log(0.2) - 1.3862944 * jax.random.uniform(key_list[2], (NXG, NY), jnp.float32) ** steps_of(key_list[2], (NXG, NY), ((0, 64),), -0.2, 0.2)), 0.05, 0.2),
        "transport_ratios": jnp.clip(jax.random.uniform(key_list[3], (2, NXG, NY), jnp.float32, -0.3, 0.3) * steps_of(key_list[3], (2, NXG, NY), ((1, 64),), -0.4, 0.0), -0.3, 0.3),
        "obs_value": scatter_about(key_list[4], (BATCHES, NOBS), 1.5, 6.0, (), jnp.float32),
        "obs_error": jnp.clip(jnp.exp(jax.random.uniform(key_list[5], (BATCHES, NOBS), jnp.float32, math.log(0.4), math.log(1.2))), 0.4, 1.2),
        "obs_noise": scatter_about(key_list[6], (BATCHES, MEMBERS, NOBS), 1.0, 6.0, (), jnp.float32),
        "obs_row": plant(jax.random.randint(key_list[7], (BATCHES, NOBS), 0, NXG), jax.random.fold_in(key_list[7], 1), 0, NXG - 1).astype(jnp.int32),
        "obs_col": plant(jax.random.randint(key_list[8], (BATCHES, NOBS), 1, NY - 1), jax.random.fold_in(key_list[8], 1), 1, (NY - 1) - 1).astype(jnp.int32),
        "obs_field": plant(jax.random.randint(key_list[9], (BATCHES, NOBS), 0, FIELDS), jax.random.fold_in(key_list[9], 1), 0, FIELDS - 1).astype(jnp.int32),
    }


def propagate_ahead(present_ensemble, spreading_coefficient, transport_ratios):
    padded = jnp.pad(present_ensemble, ((0, 0), (0, 0), (1, 1), (1, 1)))
    below = padded[:, :, 2:, 1:-1]
    above = padded[:, :, :-2, 1:-1]
    right = padded[:, :, 1:-1, 2:]
    left = padded[:, :, 1:-1, :-2]
    laplacian_operator = below + above + right + left - 4.0 * present_ensemble
    return present_ensemble + spreading_coefficient * laplacian_operator - transport_ratios[0] * (below - above) * 0.5 - transport_ratios[1] * (right - left) * 0.5

def observe(level_zero, rows, cols, fields, row_start, col_start):
    members, nfield, height, width = level_zero.shape
    flat = level_zero.reshape(members, nfield * height * width)
    total = jnp.zeros((members, rows.shape[0]), jnp.float32)
    for offset, factor in ((-1, 0.25), (0, 0.5), (1, 0.25)):
        row_within = rows - row_start
        column_within = cols + offset - col_start
        valid = (row_within >= 0) & (row_within < height) & (column_within >= 0) & (column_within < width)
        index = ((fields * height + jnp.clip(row_within, 0, height - 1)) * width + jnp.clip(column_within, 0, width - 1)).astype(jnp.int32)
        picked = jnp.take(flat, index, axis=1)
        total = total + factor * jnp.where(valid[None, :], picked, 0.0)
    return total

def transform(observed, values, errors, noise):
    members = observed.shape[0]
    rescaled_values = (observed - jnp.mean(observed, axis=0, keepdims=True)) / errors[None, :]
    innovation = (values[None, :] - observed) / errors[None, :] + noise
    eye = jnp.eye(members, dtype=jnp.float32)
    system = jnp.dot(rescaled_values.astype(jnp.float32), rescaled_values.T.astype(jnp.float32), precision=lax.Precision.HIGHEST, preferred_element_type=jnp.float32) + (members - 1.0) * eye
    right = jnp.dot(rescaled_values.astype(jnp.float32), innovation.T.astype(jnp.float32), precision=lax.Precision.HIGHEST, preferred_element_type=jnp.float32)
    factor = jnp.linalg.cholesky(system)
    middle = lax.linalg.triangular_solve(factor, right, left_side=True, lower=True)
    weights = lax.linalg.triangular_solve(factor, middle, left_side=True, lower=True, transpose_a=True)
    return eye + weights - jnp.mean(weights, axis=0, keepdims=True)

def reference(present_ensemble, delayed_ensemble, spreading_coefficient, transport_ratios, obs_value, obs_error, obs_noise, obs_row, obs_col, obs_field):
    predictive_dynamics = propagate_ahead(present_ensemble, spreading_coefficient, transport_ratios)
    flattened_system_array = jnp.concatenate([predictive_dynamics[:, None], delayed_ensemble], axis=1)
    for batch in range(BATCHES):
        observed = observe(flattened_system_array[:, 0], obs_row[batch], obs_col[batch], obs_field[batch], 0, 0)
        matrix = transform(observed, obs_value[batch], obs_error[batch], obs_noise[batch])
        flattened_system_array = jnp.einsum('jlfrn,jm->mlfrn', flattened_system_array, matrix, precision=lax.Precision.HIGHEST)
    return flattened_system_array
```

```python
import functools

import jax
import jax.numpy as jnp
from jax import lax
from jax.experimental import pallas as pl
from jax.experimental.pallas import tpu as pltpu
from jax.sharding import PartitionSpec as P

NY = 4
NC = 2
HIGHEST = lax.Precision.HIGHEST
F32 = jnp.float32
MESH = pl.DeviceIdType.MESH


def sides(x):
    rows = x.shape[0]
    row = lax.broadcasted_iota(jnp.int32, x.shape, 0) % 4
    lane = lax.broadcasted_iota(jnp.int32, x.shape, 1)
    left = pltpu.roll(x, 1, 1)
    right = pltpu.roll(x, 127, 1)
    before = jnp.where(row == 0, 0.0, pltpu.roll(left, 1, 0))
    after = jnp.where(row == 3, 0.0, pltpu.roll(right, rows - 1, 0))
    return jnp.where(lane == 0, before, left), jnp.where(lane == 127, after, right)


def gather_kernel(
    slabs,
    mems,
    cur_ref,
    delayed_ref,
    spread_ref,
    ratio_ref,
    row_ref,
    col_ref,
    field_ref,
    obs_ref,
    state_ref,
    above_ref,
    below_ref,
    fore_ref,
    smooth_ref,
    part_ref,
    ybuf,
    ysum,
    zbuf,
    zsum,
    own_ref,
    send_sem,
    recv_sem,
    local_sem,
):
    nz, nx = slabs // NY, mems // NC
    slab, mem = lax.axis_index("slab"), lax.axis_index("mem")
    z, y = slab // NY, slab % NY
    xc, core = mem // NC, mem % NC
    members, depth = cur_ref.shape[0], cur_ref.shape[1]
    rows = members * depth

    nxt = (lax.rem(slab + 1, slabs), mem)
    prv = (lax.rem(slab + slabs - 1, slabs), mem)
    ypeer = [(z * NY + lax.rem(y + d, NY), mem) for d in range(NY)]
    zpeer = [(lax.rem(z + d, nz) * NY + y, mem) for d in range(nz)]
    mpeer = [(slab, lax.rem(mem + d, mems)) for d in range(mems)]
    xpeer = [(slab, lax.rem(xc + d, nx) * NC + core) for d in range(nx)]
    twin = (slab, xc * NC + (1 - core))

    barrier = pltpu.get_barrier_semaphore()
    greeted = [nxt, prv] + ypeer[1:] + zpeer[1:] + mpeer[1:]
    for peer in greeted:
        pl.semaphore_signal(barrier, inc=1, device_id=peer, device_id_type=MESH)
    pl.semaphore_wait(barrier, len(greeted))

    used = [0]

    def send(src, dst, peer):
        k = used[0]
        used[0] += 1
        copy = pltpu.make_async_remote_copy(
            src_ref=src,
            dst_ref=dst,
            send_sem=send_sem.at[k],
            recv_sem=recv_sem.at[k],
            device_id=peer,
            device_id_type=MESH,
        )
        copy.start()
        return copy

    halo = [send(cur_ref, above_ref, nxt), send(cur_ref, below_ref, prv)]
    lagged = pl.ds(depth, delayed_ref.shape[1])
    level0 = pl.ds(0, depth)
    bulk = [send(delayed_ref, state_ref.at[mem, :, lagged, :], xpeer[d]) for d in range(1, nx)]
    keep = pltpu.make_async_copy(delayed_ref, state_ref.at[mem, :, lagged, :], local_sem.at[0])
    keep.start()

    cur = cur_ref[...].reshape(rows, 128)
    left, right = sides(cur)

    def every(c):
        block = jnp.concatenate([c] * (depth // 4), axis=0)
        return jnp.broadcast_to(block[None], (members, depth, 128)).reshape(rows, 128)

    spread = every(spread_ref[...])
    ratio0 = every(ratio_ref[0])
    ratio1 = every(ratio_ref[1])
    for copy in halo:
        copy.wait_recv()
    above = jnp.where(slab > 0, above_ref[...].reshape(rows, 128), 0.0)
    below = jnp.where(slab < slabs - 1, below_ref[...].reshape(rows, 128), 0.0)
    forecast = (
        cur
        + spread * (below + above + right + left - 4.0 * cur)
        - ratio0 * (below - above) * 0.5
        - ratio1 * (right - left) * 0.5
    )
    fore_ref[...] = forecast.reshape(members, depth, 128)
    for d in range(1, nx):
        bulk.append(send(fore_ref, state_ref.at[mem, :, level0, :], xpeer[d]))
    keep0 = pltpu.make_async_copy(fore_ref, state_ref.at[mem, :, level0, :], local_sem.at[1])
    keep0.start()

    left, right = sides(forecast)
    smooth = 0.25 * left + 0.5 * forecast + 0.25 * right
    smooth_ref[...] = smooth.reshape(members, depth, 128)
    place = jnp.where(row_ref[...] == slab, field_ref[...] * 512 + col_ref[...], -1)
    place = jnp.concatenate([place[b : b + 1] for b in range(place.shape[0])], axis=1)
    total = place.shape[1]
    spot = lax.broadcasted_iota(jnp.int32, (256, total), 0)
    acc = jnp.zeros((3 * members, total), F32)
    for g in range(depth // 2):
        values = jnp.concatenate([smooth_ref[:, 2 * g, :], smooth_ref[:, 2 * g + 1, :]], axis=1)
        high = values.astype(jnp.bfloat16).astype(F32)
        rest = values - high
        middle = rest.astype(jnp.bfloat16).astype(F32)
        low = rest - middle
        lhs = jnp.concatenate([high, middle, low], axis=0).astype(jnp.bfloat16)
        hot = jnp.where(spot + 256 * g == place, 1.0, 0.0).astype(jnp.bfloat16)
        acc = acc + jnp.dot(lhs, hot, preferred_element_type=F32)
    picked = acc[:members] + acc[members : 2 * members] + acc[2 * members :]
    for q in range(NY):
        part_ref[q] = picked[:, q * 128 : (q + 1) * 128]

    ysend = [send(part_ref.at[lax.rem(y + d, NY)], ybuf.at[d], ypeer[d]) for d in range(1, NY)]
    value = part_ref[y]
    for d, copy in enumerate(ysend, 1):
        copy.wait_recv()
        value = value + ybuf[d]
    ysum[...] = value

    zsend = [send(ysum, zbuf.at[d], zpeer[d]) for d in range(1, nz)]
    keep.wait()
    keep0.wait()
    for copy in bulk:
        copy.wait_recv()
    forward = []
    for d in range(nx):
        block = state_ref.at[lax.rem(xc + d, nx) * NC + core]
        forward.append(send(block, block, twin))

    for d, copy in enumerate(zsend, 1):
        copy.wait_recv()
        value = value + zbuf[d]
    zsum[...] = value
    own_ref[y] = value
    gathered = [send(zsum, own_ref.at[y], ypeer[d]) for d in range(1, NY)]
    for copy in gathered:
        copy.wait_recv()
    last = [send(own_ref, obs_ref.at[mem], mpeer[d]) for d in range(1, mems)]
    obs_ref[mem] = own_ref[...]
    for copy in last:
        copy.wait_recv()
    for copy in forward:
        copy.wait_recv()
    for copy in halo + bulk + ysend + zsend + forward + gathered + last:
        copy.wait_send()


def eliminate(system, n):
    row = lax.broadcasted_iota(jnp.int32, system.shape, 0)
    panel = 4
    for base in range(0, n, panel):
        columns = [
            jnp.broadcast_to(system[:, n + base + i : n + base + i + 1], system.shape)
            for i in range(panel)
        ]
        for i in range(panel):
            k = base + i
            mine = row == k
            column = columns[i]
            inverse = 1.0 / column[k : k + 1, :]
            pivot = system[k : k + 1, :] * inverse
            system = jnp.where(mine, pivot, system - column * pivot)
            for j in range(i + 1, panel):
                scale = columns[j][k : k + 1, :] * inverse
                columns[j] = jnp.where(mine, scale, columns[j] - column * scale)
    return system[:, :n]


def update_kernel(value_ref, error_ref, noise_ref, obs_ref, state_ref, out_ref, matrix_ref):
    mems, pieces, members, width = obs_ref.shape
    n = mems * members
    batches = value_ref.shape[0]
    per = pieces // batches
    eye = jnp.where(
        lax.broadcasted_iota(jnp.int32, (n, n), 0) == lax.broadcasted_iota(jnp.int32, (n, n), 1),
        1.0,
        0.0,
    )
    shifted = jnp.where(
        lax.broadcasted_iota(jnp.int32, (n, 2 * n), 0) + n
        == lax.broadcasted_iota(jnp.int32, (n, 2 * n), 1),
        n - 1.0,
        0.0,
    )
    so_far = None
    for b in range(batches):
        observed = jnp.concatenate(
            [obs_ref[:, q].reshape(n, width) for q in range(b * per, (b + 1) * per)], axis=1
        )
        if so_far is not None:
            observed = jnp.dot(so_far, observed, precision=HIGHEST, preferred_element_type=F32)
        error = error_ref[b : b + 1, :]
        scaled = (observed - jnp.mean(observed, axis=0, keepdims=True)) / error
        innovation = (value_ref[b : b + 1, :] - observed) / error + noise_ref[b]
        both = jnp.concatenate([innovation, scaled], axis=0)
        system = shifted + lax.dot_general(
            scaled, both, (((1,), (1,)), ((), ())), precision=HIGHEST, preferred_element_type=F32
        )
        weights = eliminate(system, n)
        matrix = (eye + weights - jnp.mean(weights, axis=0, keepdims=True)).T
        if so_far is None:
            so_far = matrix
        else:
            so_far = jnp.dot(matrix, so_far, precision=HIGHEST, preferred_element_type=F32)
    matrix_ref[...] = so_far
    start = pl.multiple_of(lax.axis_index("mem") * members, members)
    mine = matrix_ref[pl.ds(start, members), :]
    for t in range(0, state_ref.shape[2], 2):
        block = jnp.concatenate(
            [state_ref[:, :, t + i, :].reshape(n, 128) for i in range(2)], axis=1
        )
        result = jnp.dot(mine, block, precision=HIGHEST, preferred_element_type=F32)
        for i in range(2):
            out_ref[:, t + i, :] = result[:, i * 128 : (i + 1) * 128]


def shards(
    slabs,
    mems,
    present_ensemble,
    delayed_ensemble,
    spreading_coefficient,
    transport_ratios,
    obs_value,
    obs_error,
    obs_noise,
    obs_row,
    obs_col,
    obs_field,
):
    members, fields = present_ensemble.shape[:2]
    lags = delayed_ensemble.shape[1]
    depth = fields * 4
    levels = (lags + 1) * depth
    copies = 2 + 2 * (mems // NC - 1) + 2 * (NY - 1) + (slabs // NY - 1) + mems // NC + mems - 1
    vmem = pl.BlockSpec(memory_space=pltpu.VMEM)
    observed, state = pl.pallas_call(
        functools.partial(gather_kernel, slabs, mems),
        out_shape=(
            jax.ShapeDtypeStruct((mems, NY, members, 128), F32),
            jax.ShapeDtypeStruct((mems, members, levels, 128), F32),
        ),
        in_specs=[vmem] * 7,
        out_specs=(vmem, vmem),
        scratch_shapes=[
            pltpu.VMEM((members, depth, 128), F32),
            pltpu.VMEM((members, depth, 128), F32),
            pltpu.VMEM((members, depth, 128), F32),
            pltpu.VMEM((members, depth, 128), F32),
            pltpu.VMEM((NY, members, 128), F32),
            pltpu.VMEM((NY, members, 128), F32),
            pltpu.VMEM((members, 128), F32),
            pltpu.VMEM((slabs // NY, members, 128), F32),
            pltpu.VMEM((members, 128), F32),
            pltpu.VMEM((NY, members, 128), F32),
            pltpu.SemaphoreType.DMA((copies,)),
            pltpu.SemaphoreType.DMA((copies,)),
            pltpu.SemaphoreType.DMA((2,)),
        ],
        compiler_params=pltpu.CompilerParams(collective_id=0, has_side_effects=True),
        name="gather",
    )(
        present_ensemble.reshape(members, depth, 128),
        delayed_ensemble.reshape(members, lags * depth, 128),
        spreading_coefficient.reshape(4, 128),
        transport_ratios.reshape(2, 4, 128),
        obs_row,
        obs_col,
        obs_field,
    )
    result = pl.pallas_call(
        update_kernel,
        out_shape=jax.ShapeDtypeStruct((members, levels, 128), F32),
        in_specs=[vmem] * 5,
        out_specs=vmem,
        scratch_shapes=[pltpu.VMEM((mems * members, mems * members), F32)],
        name="update",
    )(obs_value, obs_error, obs_noise, observed, state)
    return result.reshape(members, lags + 1, fields, 1, 512)


def solution(mesh):
    slabs, mems = mesh.shape["slab"], mesh.shape["mem"]
    return jax.shard_map(
        functools.partial(shards, slabs, mems),
        mesh=mesh,
        in_specs=(
            P("mem", None, "slab", None),
            P("mem", None, None, "slab", None),
            P("slab", None),
            P(None, "slab", None),
            P(),
            P(),
            P(),
            P(),
            P(),
            P(),
        ),
        out_specs=P("mem", None, None, "slab", None),
        check_vma=False,
    )
```

```python
import functools

import jax
import jax.numpy as jnp
from jax import lax
from jax.experimental import pallas as pl
from jax.experimental.pallas import tpu as pltpu
from jax.sharding import PartitionSpec as P

NY = 4
NC = 2
HIGHEST = lax.Precision.HIGHEST
F32 = jnp.float32
MESH = pl.DeviceIdType.MESH


def sides(x):
    rows = x.shape[0]
    row = lax.broadcasted_iota(jnp.int32, x.shape, 0) % 4
    lane = lax.broadcasted_iota(jnp.int32, x.shape, 1)
    left = pltpu.roll(x, 1, 1)
    right = pltpu.roll(x, 127, 1)
    before = jnp.where(row == 0, 0.0, pltpu.roll(left, 1, 0))
    after = jnp.where(row == 3, 0.0, pltpu.roll(right, rows - 1, 0))
    return jnp.where(lane == 0, before, left), jnp.where(lane == 127, after, right)


def gather_kernel(
    slabs,
    mems,
    cur_ref,
    delayed_ref,
    spread_ref,
    ratio_ref,
    row_ref,
    col_ref,
    field_ref,
    obs_ref,
    state_ref,
    above_ref,
    below_ref,
    fore_ref,
    smooth_ref,
    part_ref,
    ybuf,
    ysum,
    zbuf,
    zsum,
    hot_ref,
    send_sem,
    recv_sem,
    local_sem,
):
    nz, nx = slabs // NY, mems // NC
    slab, mem = lax.axis_index("slab"), lax.axis_index("mem")
    z, y = slab // NY, slab % NY
    xc, core = mem // NC, mem % NC
    members, depth = cur_ref.shape[0], cur_ref.shape[1]
    rows = members * depth

    nxt = (lax.rem(slab + 1, slabs), mem)
    prv = (lax.rem(slab + slabs - 1, slabs), mem)
    ypeer = [(z * NY + lax.rem(y + d, NY), mem) for d in range(NY)]
    zpeer = [(lax.rem(z + d, nz) * NY + y, mem) for d in range(nz)]
    plane = [
        (z * NY + lax.rem(y + dy, NY), lax.rem(xc + dx, nx) * NC + core)
        for dx in range(nx)
        for dy in range(NY)
    ][1:]
    xpeer = [(slab, lax.rem(xc + d, nx) * NC + core) for d in range(nx)]
    twin = (slab, xc * NC + (1 - core))

    barrier = pltpu.get_barrier_semaphore()
    greeted = [nxt, prv, twin] + zpeer[1:] + plane
    for peer in greeted:
        pl.semaphore_signal(barrier, inc=1, device_id=peer, device_id_type=MESH)
    cur = cur_ref[...].reshape(rows, 128)
    left, right = sides(cur)

    def every(c):
        block = jnp.concatenate([c] * (depth // 4), axis=0)
        return jnp.broadcast_to(block[None], (members, depth, 128)).reshape(rows, 128)

    spread = every(spread_ref[...])
    ratio0 = every(ratio_ref[0])
    ratio1 = every(ratio_ref[1])
    inner = cur + spread * (right + left - 4.0 * cur) - ratio1 * (right - left) * 0.5
    fore_ref[...] = inner.reshape(members, depth, 128)
    from_below = spread - 0.5 * ratio0
    from_above = spread + 0.5 * ratio0
    place = jnp.where(row_ref[...] == slab, field_ref[...] * 512 + col_ref[...], -1)
    place = jnp.concatenate([place[b : b + 1] for b in range(place.shape[0])], axis=1)
    total = place.shape[1]
    spot = lax.broadcasted_iota(jnp.int32, (256, total), 0)
    for g in range(depth // 2):
        hot_ref[g] = jnp.where(spot + 256 * g == place, 1.0, 0.0).astype(jnp.bfloat16)
    pl.semaphore_wait(barrier, len(greeted))

    used = [0]

    def send(src, dst, peer):
        k = used[0]
        used[0] += 1
        copy = pltpu.make_async_remote_copy(
            src_ref=src,
            dst_ref=dst,
            send_sem=send_sem.at[k],
            recv_sem=recv_sem.at[k],
            device_id=peer,
            device_id_type=MESH,
        )
        copy.start()
        return copy

    halo = [send(cur_ref, above_ref, nxt), send(cur_ref, below_ref, prv)]
    lagged = pl.ds(depth, delayed_ref.shape[1])
    level0 = pl.ds(0, depth)
    bulk = [send(delayed_ref, state_ref.at[mem, :, lagged, :], xpeer[d]) for d in range(1, nx)]
    keep = pltpu.make_async_copy(delayed_ref, state_ref.at[mem, :, lagged, :], local_sem.at[0])
    keep.start()

    for copy in halo:
        copy.wait_recv()
    above = jnp.where(slab > 0, above_ref[...].reshape(rows, 128), 0.0)
    below = jnp.where(slab < slabs - 1, below_ref[...].reshape(rows, 128), 0.0)
    inner = fore_ref[...].reshape(rows, 128)
    forecast = inner + from_below * below + from_above * above
    fore_ref[...] = forecast.reshape(members, depth, 128)
    for d in range(1, nx):
        bulk.append(send(fore_ref, state_ref.at[mem, :, level0, :], xpeer[d]))
    keep0 = pltpu.make_async_copy(fore_ref, state_ref.at[mem, :, level0, :], local_sem.at[1])
    keep0.start()

    left, right = sides(forecast)
    smooth = 0.25 * left + 0.5 * forecast + 0.25 * right
    smooth_ref[...] = smooth.reshape(members, depth, 128)
    acc = jnp.zeros((3 * members, total), F32)
    for g in range(depth // 2):
        values = jnp.concatenate([smooth_ref[:, 2 * g, :], smooth_ref[:, 2 * g + 1, :]], axis=1)
        high = values.astype(jnp.bfloat16).astype(F32)
        rest = values - high
        middle = rest.astype(jnp.bfloat16).astype(F32)
        low = rest - middle
        lhs = jnp.concatenate([high, middle, low], axis=0).astype(jnp.bfloat16)
        acc = acc + jnp.dot(lhs, hot_ref[g], preferred_element_type=F32)
    picked = acc[:members] + acc[members : 2 * members] + acc[2 * members :]
    for q in range(NY):
        part_ref[q] = picked[:, q * 128 : (q + 1) * 128]

    ysend = [send(part_ref.at[lax.rem(y + d, NY)], ybuf.at[d], ypeer[d]) for d in range(1, NY)]
    value = part_ref[y]
    for d, copy in enumerate(ysend, 1):
        copy.wait_recv()
        value = value + ybuf[d]
    ysum[...] = value

    far = sorted(range(1, nz), key=lambda d: -min(d, nz - d))
    zsend = [send(ysum, zbuf.at[d], zpeer[d]) for d in far]
    keep.wait()
    keep0.wait()
    for copy in bulk:
        copy.wait_recv()
    forward = []
    for d in range(nx):
        block = state_ref.at[lax.rem(xc + d, nx) * NC + core]
        forward.append(send(block, block, twin))

    for d, copy in reversed(list(zip(far, zsend))):
        copy.wait_recv()
        value = value + zbuf[d]
    zsum[...] = value
    obs_ref[mem, y] = value
    tiles = [send(zsum, obs_ref.at[mem, y], peer) for peer in plane]
    for copy in tiles:
        copy.wait_recv()
    last = []
    for d in range(nx):
        block = obs_ref.at[lax.rem(xc + d, nx) * NC + core]
        last.append(send(block, block, twin))
    for copy in last:
        copy.wait_recv()
    for copy in forward:
        copy.wait_recv()
    for copy in halo + bulk + ysend + zsend + forward + tiles + last:
        copy.wait_send()


def eliminate(system, n):
    row = lax.broadcasted_iota(jnp.int32, system.shape, 0)
    panel = 4
    for base in range(0, n, panel):
        columns = [
            jnp.broadcast_to(system[:, n + base + i : n + base + i + 1], system.shape)
            for i in range(panel)
        ]
        for i in range(panel):
            k = base + i
            mine = row == k
            column = columns[i]
            inverse = 1.0 / column[k : k + 1, :]
            pivot = system[k : k + 1, :] * inverse
            system = jnp.where(mine, pivot, system - column * pivot)
            for j in range(i + 1, panel):
                scale = columns[j][k : k + 1, :] * inverse
                columns[j] = jnp.where(mine, scale, columns[j] - column * scale)
    return system[:, :n]


def update_kernel(value_ref, error_ref, noise_ref, obs_ref, state_hbm, out_ref, matrix_ref, state_ref, load_sem):
    load = pltpu.make_async_copy(state_hbm, state_ref, load_sem)
    load.start()
    mems, pieces, members, width = obs_ref.shape
    n = mems * members
    batches = value_ref.shape[0]
    per = pieces // batches
    eye = jnp.where(
        lax.broadcasted_iota(jnp.int32, (n, n), 0) == lax.broadcasted_iota(jnp.int32, (n, n), 1),
        1.0,
        0.0,
    )
    shifted = jnp.where(
        lax.broadcasted_iota(jnp.int32, (n, 2 * n), 0) + n
        == lax.broadcasted_iota(jnp.int32, (n, 2 * n), 1),
        n - 1.0,
        0.0,
    )
    so_far = None
    for b in range(batches):
        observed = jnp.concatenate(
            [obs_ref[:, q].reshape(n, width) for q in range(b * per, (b + 1) * per)], axis=1
        )
        if so_far is not None:
            observed = jnp.dot(so_far, observed, precision=HIGHEST, preferred_element_type=F32)
        error = error_ref[b : b + 1, :]
        scaled = (observed - jnp.mean(observed, axis=0, keepdims=True)) / error
        innovation = (value_ref[b : b + 1, :] - observed) / error + noise_ref[b]
        both = jnp.concatenate([innovation, scaled], axis=0)
        system = shifted + lax.dot_general(
            scaled, both, (((1,), (1,)), ((), ())), precision=HIGHEST, preferred_element_type=F32
        )
        weights = eliminate(system, n)
        matrix = (eye + weights - jnp.mean(weights, axis=0, keepdims=True)).T
        if so_far is None:
            so_far = matrix
        else:
            so_far = jnp.dot(matrix, so_far, precision=HIGHEST, preferred_element_type=F32)
    matrix_ref[...] = so_far
    start = pl.multiple_of(lax.axis_index("mem") * members, members)
    mine = matrix_ref[pl.ds(start, members), :]
    load.wait()
    for t in range(0, state_ref.shape[2], 2):
        block = jnp.concatenate(
            [state_ref[:, :, t + i, :].reshape(n, 128) for i in range(2)], axis=1
        )
        result = jnp.dot(mine, block, precision=HIGHEST, preferred_element_type=F32)
        for i in range(2):
            out_ref[:, t + i, :] = result[:, i * 128 : (i + 1) * 128]


def shards(
    slabs,
    mems,
    present_ensemble,
    delayed_ensemble,
    spreading_coefficient,
    transport_ratios,
    obs_value,
    obs_error,
    obs_noise,
    obs_row,
    obs_col,
    obs_field,
):
    members, fields = present_ensemble.shape[:2]
    lags = delayed_ensemble.shape[1]
    depth = fields * 4
    levels = (lags + 1) * depth
    nx = mems // NC
    copies = 2 + 2 * (nx - 1) + (NY - 1) + (slabs // NY - 1) + (NY * nx - 1) + 2 * nx
    vmem = pl.BlockSpec(memory_space=pltpu.VMEM)
    observed, state = pl.pallas_call(
        functools.partial(gather_kernel, slabs, mems),
        out_shape=(
            jax.ShapeDtypeStruct((mems, NY, members, 128), F32),
            jax.ShapeDtypeStruct((mems, members, levels, 128), F32),
        ),
        in_specs=[vmem] * 7,
        out_specs=(vmem, pl.BlockSpec(memory_space=pl.ANY)),
        scratch_shapes=[
            pltpu.VMEM((members, depth, 128), F32),
            pltpu.VMEM((members, depth, 128), F32),
            pltpu.VMEM((members, depth, 128), F32),
            pltpu.VMEM((members, depth, 128), F32),
            pltpu.VMEM((NY, members, 128), F32),
            pltpu.VMEM((NY, members, 128), F32),
            pltpu.VMEM((members, 128), F32),
            pltpu.VMEM((slabs // NY, members, 128), F32),
            pltpu.VMEM((members, 128), F32),
            pltpu.VMEM((depth // 2, 256, obs_row.size), jnp.bfloat16),
            pltpu.SemaphoreType.DMA((copies,)),
            pltpu.SemaphoreType.DMA((copies,)),
            pltpu.SemaphoreType.DMA((2,)),
        ],
        compiler_params=pltpu.CompilerParams(collective_id=0, has_side_effects=True),
        name="gather",
    )(
        present_ensemble.reshape(members, depth, 128),
        delayed_ensemble.reshape(members, lags * depth, 128),
        spreading_coefficient.reshape(4, 128),
        transport_ratios.reshape(2, 4, 128),
        obs_row,
        obs_col,
        obs_field,
    )
    result = pl.pallas_call(
        update_kernel,
        out_shape=jax.ShapeDtypeStruct((members, levels, 128), F32),
        in_specs=[vmem] * 4 + [pl.BlockSpec(memory_space=pl.ANY)],
        out_specs=vmem,
        scratch_shapes=[
            pltpu.VMEM((mems * members, mems * members), F32),
            pltpu.VMEM((mems, members, levels, 128), F32),
            pltpu.SemaphoreType.DMA,
        ],
        name="update",
    )(obs_value, obs_error, obs_noise, observed, state)
    return result.reshape(members, lags + 1, fields, 1, 512)


def solution(mesh):
    slabs, mems = mesh.shape["slab"], mesh.shape["mem"]
    return jax.shard_map(
        functools.partial(shards, slabs, mems),
        mesh=mesh,
        in_specs=(
            P("mem", None, "slab", None),
            P("mem", None, None, "slab", None),
            P("slab", None),
            P(None, "slab", None),
            P(),
            P(),
            P(),
            P(),
            P(),
            P(),
        ),
        out_specs=P("mem", None, None, "slab", None),
        check_vma=False,
    )
```

```python
import functools

import jax
import jax.numpy as jnp
from jax import lax
from jax.experimental import pallas as pl
from jax.experimental.pallas import tpu as pltpu
from jax.sharding import PartitionSpec as P

NY = 4
NC = 2
HIGHEST = lax.Precision.HIGHEST
F32 = jnp.float32
MESH = pl.DeviceIdType.MESH


def sides(x):
    rows = x.shape[0]
    row = lax.broadcasted_iota(jnp.int32, x.shape, 0) % 4
    lane = lax.broadcasted_iota(jnp.int32, x.shape, 1)
    left = pltpu.roll(x, 1, 1)
    right = pltpu.roll(x, 127, 1)
    before = jnp.where(row == 0, 0.0, pltpu.roll(left, 1, 0))
    after = jnp.where(row == 3, 0.0, pltpu.roll(right, rows - 1, 0))
    return jnp.where(lane == 0, before, left), jnp.where(lane == 127, after, right)


def window_kernel(
    slabs,
    mems,
    cur_ref,
    delayed_ref,
    spread_ref,
    ratio_ref,
    row_ref,
    col_ref,
    field_ref,
    value_ref,
    error_ref,
    noise_ref,
    out_ref,
    obs_ref,
    state_ref,
    matrix_ref,
    above_ref,
    below_ref,
    fore_ref,
    smooth_ref,
    part_ref,
    ybuf,
    ysum,
    zbuf,
    zsum,
    hot_ref,
    send_sem,
    recv_sem,
    local_sem,
):
    nz, nx = slabs // NY, mems // NC
    slab, mem = lax.axis_index("slab"), lax.axis_index("mem")
    z, y = slab // NY, slab % NY
    xc, core = mem // NC, mem % NC
    members, depth = cur_ref.shape[0], cur_ref.shape[1]
    rows = members * depth

    nxt = (lax.rem(slab + 1, slabs), mem)
    prv = (lax.rem(slab + slabs - 1, slabs), mem)
    ypeer = [(z * NY + lax.rem(y + d, NY), mem) for d in range(NY)]
    zpeer = [(lax.rem(z + d, nz) * NY + y, mem) for d in range(nz)]
    plane = [
        (z * NY + lax.rem(y + dy, NY), lax.rem(xc + dx, nx) * NC + core)
        for dx in range(nx)
        for dy in range(NY)
    ][1:]
    xpeer = [(slab, lax.rem(xc + d, nx) * NC + core) for d in range(nx)]
    twin = (slab, xc * NC + (1 - core))

    barrier = pltpu.get_barrier_semaphore()
    greeted = [nxt, prv, twin] + zpeer[1:] + plane
    for peer in greeted:
        pl.semaphore_signal(barrier, inc=1, device_id=peer, device_id_type=MESH)
    cur = cur_ref[...].reshape(rows, 128)
    left, right = sides(cur)

    def every(c):
        block = jnp.concatenate([c] * (depth // 4), axis=0)
        return jnp.broadcast_to(block[None], (members, depth, 128)).reshape(rows, 128)

    spread = every(spread_ref[...])
    ratio0 = every(ratio_ref[0])
    ratio1 = every(ratio_ref[1])
    inner = cur + spread * (right + left - 4.0 * cur) - ratio1 * (right - left) * 0.5
    fore_ref[...] = inner.reshape(members, depth, 128)
    from_below = spread - 0.5 * ratio0
    from_above = spread + 0.5 * ratio0
    place = jnp.where(row_ref[...] == slab, field_ref[...] * 512 + col_ref[...], -1)
    place = jnp.concatenate([place[b : b + 1] for b in range(place.shape[0])], axis=1)
    total = place.shape[1]
    spot = lax.broadcasted_iota(jnp.int32, (256, total), 0)
    for g in range(depth // 2):
        hot_ref[g] = jnp.where(spot + 256 * g == place, 1.0, 0.0).astype(jnp.bfloat16)
    pl.semaphore_wait(barrier, len(greeted))

    used = [0]

    def send(src, dst, peer):
        k = used[0]
        used[0] += 1
        copy = pltpu.make_async_remote_copy(
            src_ref=src,
            dst_ref=dst,
            send_sem=send_sem.at[k],
            recv_sem=recv_sem.at[k],
            device_id=peer,
            device_id_type=MESH,
        )
        copy.start()
        return copy

    halo = [send(cur_ref, above_ref, nxt), send(cur_ref, below_ref, prv)]
    lagged = pl.ds(depth, delayed_ref.shape[1])
    level0 = pl.ds(0, depth)
    bulk = [send(delayed_ref, state_ref.at[mem, :, lagged, :], xpeer[d]) for d in range(1, nx)]
    keep = pltpu.make_async_copy(delayed_ref, state_ref.at[mem, :, lagged, :], local_sem.at[0])
    keep.start()

    for copy in halo:
        copy.wait_recv()
    above = jnp.where(slab > 0, above_ref[...].reshape(rows, 128), 0.0)
    below = jnp.where(slab < slabs - 1, below_ref[...].reshape(rows, 128), 0.0)
    inner = fore_ref[...].reshape(rows, 128)
    forecast = inner + from_below * below + from_above * above
    fore_ref[...] = forecast.reshape(members, depth, 128)
    for d in range(1, nx):
        bulk.append(send(fore_ref, state_ref.at[mem, :, level0, :], xpeer[d]))
    keep0 = pltpu.make_async_copy(fore_ref, state_ref.at[mem, :, level0, :], local_sem.at[1])
    keep0.start()

    left, right = sides(forecast)
    smooth = 0.25 * left + 0.5 * forecast + 0.25 * right
    smooth_ref[...] = smooth.reshape(members, depth, 128)
    acc = jnp.zeros((3 * members, total), F32)
    for g in range(depth // 2):
        values = jnp.concatenate([smooth_ref[:, 2 * g, :], smooth_ref[:, 2 * g + 1, :]], axis=1)
        high = values.astype(jnp.bfloat16).astype(F32)
        rest = values - high
        middle = rest.astype(jnp.bfloat16).astype(F32)
        low = rest - middle
        lhs = jnp.concatenate([high, middle, low], axis=0).astype(jnp.bfloat16)
        acc = acc + jnp.dot(lhs, hot_ref[g], preferred_element_type=F32)
    picked = acc[:members] + acc[members : 2 * members] + acc[2 * members :]
    for q in range(NY):
        part_ref[q] = picked[:, q * 128 : (q + 1) * 128]

    ysend = [send(part_ref.at[lax.rem(y + d, NY)], ybuf.at[d], ypeer[d]) for d in range(1, NY)]
    value = part_ref[y]
    for d, copy in enumerate(ysend, 1):
        copy.wait_recv()
        value = value + ybuf[d]
    ysum[...] = value

    far = sorted(range(1, nz), key=lambda d: -min(d, nz - d))
    zsend = [send(ysum, zbuf.at[d], zpeer[d]) for d in far]
    keep.wait()
    keep0.wait()
    for copy in bulk:
        copy.wait_recv()
    forward = []
    for d in range(nx):
        block = state_ref.at[lax.rem(xc + d, nx) * NC + core]
        forward.append(send(block, block, twin))

    for d, copy in reversed(list(zip(far, zsend))):
        copy.wait_recv()
        value = value + zbuf[d]
    zsum[...] = value
    obs_ref[mem, y] = value
    tiles = [send(zsum, obs_ref.at[mem, y], peer) for peer in plane]
    for copy in tiles:
        copy.wait_recv()
    last = []
    for d in range(nx):
        block = obs_ref.at[lax.rem(xc + d, nx) * NC + core]
        last.append(send(block, block, twin))
    for copy in last:
        copy.wait_recv()
    matrix_ref[...] = solve(value_ref, error_ref, noise_ref, obs_ref)
    for copy in forward:
        copy.wait_recv()
    apply(mem, matrix_ref, state_ref, out_ref)
    for copy in halo + bulk + ysend + zsend + forward + tiles + last:
        copy.wait_send()


def eliminate(system, n):
    row = lax.broadcasted_iota(jnp.int32, system.shape, 0)
    panel = 4
    for base in range(0, n, panel):
        columns = [
            jnp.broadcast_to(system[:, n + base + i : n + base + i + 1], system.shape)
            for i in range(panel)
        ]
        for i in range(panel):
            k = base + i
            mine = row == k
            column = columns[i]
            inverse = 1.0 / column[k : k + 1, :]
            pivot = system[k : k + 1, :] * inverse
            system = jnp.where(mine, pivot, system - column * pivot)
            for j in range(i + 1, panel):
                scale = columns[j][k : k + 1, :] * inverse
                columns[j] = jnp.where(mine, scale, columns[j] - column * scale)
    return system[:, :n]


def solve(value_ref, error_ref, noise_ref, obs_ref):
    mems, pieces, members, width = obs_ref.shape
    n = mems * members
    batches = value_ref.shape[0]
    per = pieces // batches
    eye = jnp.where(
        lax.broadcasted_iota(jnp.int32, (n, n), 0) == lax.broadcasted_iota(jnp.int32, (n, n), 1),
        1.0,
        0.0,
    )
    shifted = jnp.where(
        lax.broadcasted_iota(jnp.int32, (n, 2 * n), 0) + n
        == lax.broadcasted_iota(jnp.int32, (n, 2 * n), 1),
        n - 1.0,
        0.0,
    )
    so_far = None
    for b in range(batches):
        observed = jnp.concatenate(
            [obs_ref[:, q].reshape(n, width) for q in range(b * per, (b + 1) * per)], axis=1
        )
        if so_far is not None:
            observed = jnp.dot(so_far, observed, precision=HIGHEST, preferred_element_type=F32)
        error = error_ref[b : b + 1, :]
        scaled = (observed - jnp.mean(observed, axis=0, keepdims=True)) / error
        innovation = (value_ref[b : b + 1, :] - observed) / error + noise_ref[b]
        both = jnp.concatenate([innovation, scaled], axis=0)
        system = shifted + lax.dot_general(
            scaled, both, (((1,), (1,)), ((), ())), precision=HIGHEST, preferred_element_type=F32
        )
        weights = eliminate(system, n)
        matrix = (eye + weights - jnp.mean(weights, axis=0, keepdims=True)).T
        if so_far is None:
            so_far = matrix
        else:
            so_far = jnp.dot(matrix, so_far, precision=HIGHEST, preferred_element_type=F32)
    return so_far


def split(x):
    high = x.astype(jnp.bfloat16)
    return high, (x - high.astype(F32)).astype(jnp.bfloat16)


def apply(mem, matrix_ref, state_ref, out_ref):
    mems, members, levels = state_ref.shape[:3]
    n = mems * members
    high, low = split(matrix_ref[pl.ds(pl.multiple_of(mem * members, members), members), :])
    lhs = jnp.concatenate([high.astype(F32), low.astype(F32), high.astype(F32)], axis=1)
    lhs = lhs.astype(jnp.bfloat16)
    for t in range(0, levels, 2):
        block = jnp.concatenate(
            [state_ref[:, :, t + i, :].reshape(n, 128) for i in range(2)], axis=1
        )
        high, low = split(block)
        rhs = jnp.concatenate([high, high, low], axis=0)
        result = jnp.dot(lhs, rhs, preferred_element_type=F32)
        for i in range(2):
            out_ref[:, t + i, :] = result[:, i * 128 : (i + 1) * 128]


def shards(
    slabs,
    mems,
    present_ensemble,
    delayed_ensemble,
    spreading_coefficient,
    transport_ratios,
    obs_value,
    obs_error,
    obs_noise,
    obs_row,
    obs_col,
    obs_field,
):
    members, fields = present_ensemble.shape[:2]
    lags = delayed_ensemble.shape[1]
    depth = fields * 4
    levels = (lags + 1) * depth
    nx = mems // NC
    copies = 2 + 2 * (nx - 1) + (NY - 1) + (slabs // NY - 1) + (NY * nx - 1) + 2 * nx
    vmem = pl.BlockSpec(memory_space=pltpu.VMEM)
    n = mems * members
    result = pl.pallas_call(
        functools.partial(window_kernel, slabs, mems),
        out_shape=jax.ShapeDtypeStruct((members, levels, 128), F32),
        in_specs=[vmem] * 10,
        out_specs=vmem,
        scratch_shapes=[
            pltpu.VMEM((mems, NY, members, 128), F32),
            pltpu.VMEM((mems, members, levels, 128), F32),
            pltpu.VMEM((n, n), F32),
            pltpu.VMEM((members, depth, 128), F32),
            pltpu.VMEM((members, depth, 128), F32),
            pltpu.VMEM((members, depth, 128), F32),
            pltpu.VMEM((members, depth, 128), F32),
            pltpu.VMEM((NY, members, 128), F32),
            pltpu.VMEM((NY, members, 128), F32),
            pltpu.VMEM((members, 128), F32),
            pltpu.VMEM((slabs // NY, members, 128), F32),
            pltpu.VMEM((members, 128), F32),
            pltpu.VMEM((depth // 2, 256, obs_row.size), jnp.bfloat16),
            pltpu.SemaphoreType.DMA((copies,)),
            pltpu.SemaphoreType.DMA((copies,)),
            pltpu.SemaphoreType.DMA((2,)),
        ],
        compiler_params=pltpu.CompilerParams(collective_id=0, has_side_effects=True),
        name="window",
    )(
        present_ensemble.reshape(members, depth, 128),
        delayed_ensemble.reshape(members, lags * depth, 128),
        spreading_coefficient.reshape(4, 128),
        transport_ratios.reshape(2, 4, 128),
        obs_row,
        obs_col,
        obs_field,
        obs_value,
        obs_error,
        obs_noise,
    )
    return result.reshape(members, lags + 1, fields, 1, 512)


def solution(mesh):
    slabs, mems = mesh.shape["slab"], mesh.shape["mem"]
    return jax.shard_map(
        functools.partial(shards, slabs, mems),
        mesh=mesh,
        in_specs=(
            P("mem", None, "slab", None),
            P("mem", None, None, "slab", None),
            P("slab", None),
            P(None, "slab", None),
            P(),
            P(),
            P(),
            P(),
            P(),
            P(),
        ),
        out_specs=P("mem", None, None, "slab", None),
        check_vma=False,
    )
```

```python
import functools

import jax
import jax.numpy as jnp
from jax import lax
from jax.experimental import pallas as pl
from jax.experimental.pallas import tpu as pltpu
from jax.sharding import PartitionSpec as P

NY = 4
NC = 2
HIGHEST = lax.Precision.HIGHEST
F32 = jnp.float32
MESH = pl.DeviceIdType.MESH


def sides(x):
    rows = x.shape[0]
    row = lax.broadcasted_iota(jnp.int32, x.shape, 0) % 4
    lane = lax.broadcasted_iota(jnp.int32, x.shape, 1)
    left = pltpu.roll(x, 1, 1)
    right = pltpu.roll(x, 127, 1)
    before = jnp.where(row == 0, 0.0, pltpu.roll(left, 1, 0))
    after = jnp.where(row == 3, 0.0, pltpu.roll(right, rows - 1, 0))
    return jnp.where(lane == 0, before, left), jnp.where(lane == 127, after, right)


def gather_kernel(
    slabs,
    mems,
    cur_ref,
    delayed_ref,
    spread_ref,
    ratio_ref,
    row_ref,
    col_ref,
    field_ref,
    obs_ref,
    state_ref,
    above_ref,
    below_ref,
    fore_ref,
    smooth_ref,
    part_ref,
    ybuf,
    ysum,
    zbuf,
    zsum,
    hot_ref,
    send_sem,
    recv_sem,
    local_sem,
):
    nz, nx = slabs // NY, mems // NC
    slab, mem = lax.axis_index("slab"), lax.axis_index("mem")
    z, y = slab // NY, slab % NY
    xc, core = mem // NC, mem % NC
    members, depth = cur_ref.shape[0], cur_ref.shape[1]
    rows = members * depth

    nxt = (lax.rem(slab + 1, slabs), mem)
    prv = (lax.rem(slab + slabs - 1, slabs), mem)
    ypeer = [(z * NY + lax.rem(y + d, NY), mem) for d in range(NY)]
    zpeer = [(lax.rem(z + d, nz) * NY + y, mem) for d in range(nz)]
    plane = [
        (z * NY + lax.rem(y + dy, NY), lax.rem(mem + dm, mems))
        for dm in range(mems)
        for dy in range(NY)
    ][1:]
    xpeer = [(slab, lax.rem(xc + d, nx) * NC + core) for d in range(nx)]
    twin = (slab, xc * NC + (1 - core))

    barrier = pltpu.get_barrier_semaphore()
    greeted = [nxt, prv] + zpeer[1:] + plane
    for peer in greeted:
        pl.semaphore_signal(barrier, inc=1, device_id=peer, device_id_type=MESH)
    cur = cur_ref[...].reshape(rows, 128)
    left, right = sides(cur)

    def every(c):
        block = jnp.concatenate([c] * (depth // 4), axis=0)
        return jnp.broadcast_to(block[None], (members, depth, 128)).reshape(rows, 128)

    spread = every(spread_ref[...])
    ratio0 = every(ratio_ref[0])
    ratio1 = every(ratio_ref[1])
    inner = cur + spread * (right + left - 4.0 * cur) - ratio1 * (right - left) * 0.5
    fore_ref[...] = inner.reshape(members, depth, 128)
    from_below = spread - 0.5 * ratio0
    from_above = spread + 0.5 * ratio0
    place = jnp.where(row_ref[...] == slab, field_ref[...] * 512 + col_ref[...], -1)
    place = jnp.concatenate([place[b : b + 1] for b in range(place.shape[0])], axis=1)
    total = place.shape[1]
    spot = lax.broadcasted_iota(jnp.int32, (256, total), 0)
    for g in range(depth // 2):
        hot_ref[g] = jnp.where(spot + 256 * g == place, 1.0, 0.0).astype(jnp.bfloat16)
    pl.semaphore_wait(barrier, len(greeted))

    used = [0]

    def send(src, dst, peer):
        k = used[0]
        used[0] += 1
        copy = pltpu.make_async_remote_copy(
            src_ref=src,
            dst_ref=dst,
            send_sem=send_sem.at[k],
            recv_sem=recv_sem.at[k],
            device_id=peer,
            device_id_type=MESH,
        )
        copy.start()
        return copy

    halo = [send(cur_ref, above_ref, nxt), send(cur_ref, below_ref, prv)]
    lagged = pl.ds(depth, delayed_ref.shape[1])
    level0 = pl.ds(0, depth)
    bulk = [send(delayed_ref, state_ref.at[mem, :, lagged, :], xpeer[d]) for d in range(1, nx)]
    keep = pltpu.make_async_copy(delayed_ref, state_ref.at[mem, :, lagged, :], local_sem.at[0])
    keep.start()

    for copy in halo:
        copy.wait_recv()
    above = jnp.where(slab > 0, above_ref[...].reshape(rows, 128), 0.0)
    below = jnp.where(slab < slabs - 1, below_ref[...].reshape(rows, 128), 0.0)
    inner = fore_ref[...].reshape(rows, 128)
    forecast = inner + from_below * below + from_above * above
    fore_ref[...] = forecast.reshape(members, depth, 128)
    for d in range(1, nx):
        bulk.append(send(fore_ref, state_ref.at[mem, :, level0, :], xpeer[d]))
    keep0 = pltpu.make_async_copy(fore_ref, state_ref.at[mem, :, level0, :], local_sem.at[1])
    keep0.start()

    left, right = sides(forecast)
    smooth = 0.25 * left + 0.5 * forecast + 0.25 * right
    smooth_ref[...] = smooth.reshape(members, depth, 128)
    acc = jnp.zeros((3 * members, total), F32)
    for g in range(depth // 2):
        values = jnp.concatenate([smooth_ref[:, 2 * g, :], smooth_ref[:, 2 * g + 1, :]], axis=1)
        high = values.astype(jnp.bfloat16).astype(F32)
        rest = values - high
        middle = rest.astype(jnp.bfloat16).astype(F32)
        low = rest - middle
        lhs = jnp.concatenate([high, middle, low], axis=0).astype(jnp.bfloat16)
        acc = acc + jnp.dot(lhs, hot_ref[g], preferred_element_type=F32)
    picked = acc[:members] + acc[members : 2 * members] + acc[2 * members :]
    for q in range(NY):
        part_ref[q] = picked[:, q * 128 : (q + 1) * 128]

    ysend = [send(part_ref.at[lax.rem(y + d, NY)], ybuf.at[d], ypeer[d]) for d in range(1, NY)]
    value = part_ref[y]
    for d, copy in enumerate(ysend, 1):
        copy.wait_recv()
        value = value + ybuf[d]
    ysum[...] = value

    far = sorted(range(1, nz), key=lambda d: -min(d, nz - d))
    zsend = [send(ysum, zbuf.at[d], zpeer[d]) for d in far]
    keep.wait()
    keep0.wait()
    for copy in bulk:
        copy.wait_recv()
    forward = []
    for d in range(nx):
        block = state_ref.at[lax.rem(xc + d, nx) * NC + core]
        forward.append(send(block, block, twin))

    for d, copy in reversed(list(zip(far, zsend))):
        copy.wait_recv()
        value = value + zbuf[d]
    zsum[...] = value
    obs_ref[mem, y] = value
    tiles = [send(zsum, obs_ref.at[mem, y], peer) for peer in plane]
    for copy in tiles:
        copy.wait_recv()
    for copy in forward:
        copy.wait_recv()
    for copy in halo + bulk + ysend + zsend + forward + tiles:
        copy.wait_send()


def eliminate(system, n):
    row = lax.broadcasted_iota(jnp.int32, system.shape, 0)
    panel = 8
    for base in range(0, n, panel):
        columns = [
            jnp.broadcast_to(system[:, n + base + i : n + base + i + 1], system.shape)
            for i in range(panel)
        ]
        for i in range(panel):
            k = base + i
            mine = row == k
            column = columns[i]
            inverse = 1.0 / column[k : k + 1, :]
            pivot = system[k : k + 1, :] * inverse
            system = jnp.where(mine, pivot, system - column * pivot)
            for j in range(i + 1, panel):
                scale = columns[j][k : k + 1, :] * inverse
                columns[j] = jnp.where(mine, scale, columns[j] - column * scale)
    return system[:, :n]


def split(x):
    high = x.astype(jnp.bfloat16)
    return high, (x - high.astype(F32)).astype(jnp.bfloat16)


def update_kernel(value_ref, error_ref, noise_ref, obs_ref, state_hbm, out_ref, matrix_ref, state_ref, load_sem):
    load = pltpu.make_async_copy(state_hbm, state_ref, load_sem)
    load.start()
    mems, pieces, members, width = obs_ref.shape
    n = mems * members
    batches = value_ref.shape[0]
    per = pieces // batches
    eye = jnp.where(
        lax.broadcasted_iota(jnp.int32, (n, n), 0) == lax.broadcasted_iota(jnp.int32, (n, n), 1),
        1.0,
        0.0,
    )
    shifted = jnp.where(
        lax.broadcasted_iota(jnp.int32, (n, 2 * n), 0) + n
        == lax.broadcasted_iota(jnp.int32, (n, 2 * n), 1),
        n - 1.0,
        0.0,
    )
    so_far = None
    for b in range(batches):
        observed = jnp.concatenate(
            [obs_ref[:, q].reshape(n, width) for q in range(b * per, (b + 1) * per)], axis=1
        )
        if so_far is not None:
            observed = jnp.dot(so_far, observed, precision=HIGHEST, preferred_element_type=F32)
        error = error_ref[b : b + 1, :]
        scaled = (observed - jnp.mean(observed, axis=0, keepdims=True)) / error
        innovation = (value_ref[b : b + 1, :] - observed) / error + noise_ref[b]
        both = jnp.concatenate([innovation, scaled], axis=0)
        system = shifted + lax.dot_general(
            scaled, both, (((1,), (1,)), ((), ())), precision=HIGHEST, preferred_element_type=F32
        )
        weights = eliminate(system, n)
        matrix = (eye + weights - jnp.mean(weights, axis=0, keepdims=True)).T
        if so_far is None:
            so_far = matrix
        else:
            so_far = jnp.dot(matrix, so_far, precision=HIGHEST, preferred_element_type=F32)
    matrix_ref[...] = so_far
    start = pl.multiple_of(lax.axis_index("mem") * members, members)
    mine = matrix_ref[pl.ds(start, members), :]
    high, low = split(mine)
    lhs = jnp.concatenate([high.astype(F32), low.astype(F32), high.astype(F32)], axis=1)
    lhs = lhs.astype(jnp.bfloat16)
    load.wait()
    for t in range(0, state_ref.shape[2], 2):
        block = jnp.concatenate(
            [state_ref[:, :, t + i, :].reshape(n, 128) for i in range(2)], axis=1
        )
        high, low = split(block)
        rhs = jnp.concatenate([high, high, low], axis=0)
        result = jnp.dot(lhs, rhs, preferred_element_type=F32)
        for i in range(2):
            out_ref[:, t + i, :] = result[:, i * 128 : (i + 1) * 128]


def shards(
    slabs,
    mems,
    present_ensemble,
    delayed_ensemble,
    spreading_coefficient,
    transport_ratios,
    obs_value,
    obs_error,
    obs_noise,
    obs_row,
    obs_col,
    obs_field,
):
    members, fields = present_ensemble.shape[:2]
    lags = delayed_ensemble.shape[1]
    depth = fields * 4
    levels = (lags + 1) * depth
    nx = mems // NC
    copies = 2 + 2 * (nx - 1) + (NY - 1) + (slabs // NY - 1) + (NY * mems - 1) + nx
    vmem = pl.BlockSpec(memory_space=pltpu.VMEM)
    observed, state = pl.pallas_call(
        functools.partial(gather_kernel, slabs, mems),
        out_shape=(
            jax.ShapeDtypeStruct((mems, NY, members, 128), F32),
            jax.ShapeDtypeStruct((mems, members, levels, 128), F32),
        ),
        in_specs=[vmem] * 7,
        out_specs=(vmem, pl.BlockSpec(memory_space=pl.ANY)),
        scratch_shapes=[
            pltpu.VMEM((members, depth, 128), F32),
            pltpu.VMEM((members, depth, 128), F32),
            pltpu.VMEM((members, depth, 128), F32),
            pltpu.VMEM((members, depth, 128), F32),
            pltpu.VMEM((NY, members, 128), F32),
            pltpu.VMEM((NY, members, 128), F32),
            pltpu.VMEM((members, 128), F32),
            pltpu.VMEM((slabs // NY, members, 128), F32),
            pltpu.VMEM((members, 128), F32),
            pltpu.VMEM((depth // 2, 256, obs_row.size), jnp.bfloat16),
            pltpu.SemaphoreType.DMA((copies,)),
            pltpu.SemaphoreType.DMA((copies,)),
            pltpu.SemaphoreType.DMA((2,)),
        ],
        compiler_params=pltpu.CompilerParams(collective_id=0, has_side_effects=True),
        name="gather",
    )(
        present_ensemble.reshape(members, depth, 128),
        delayed_ensemble.reshape(members, lags * depth, 128),
        spreading_coefficient.reshape(4, 128),
        transport_ratios.reshape(2, 4, 128),
        obs_row,
        obs_col,
        obs_field,
    )
    result = pl.pallas_call(
        update_kernel,
        out_shape=jax.ShapeDtypeStruct((members, levels, 128), F32),
        in_specs=[vmem] * 4 + [pl.BlockSpec(memory_space=pl.ANY)],
        out_specs=vmem,
        scratch_shapes=[
            pltpu.VMEM((mems * members, mems * members), F32),
            pltpu.VMEM((mems, members, levels, 128), F32),
            pltpu.SemaphoreType.DMA,
        ],
        name="update",
    )(obs_value, obs_error, obs_noise, observed, state)
    return result.reshape(members, lags + 1, fields, 1, 512)


def solution(mesh):
    slabs, mems = mesh.shape["slab"], mesh.shape["mem"]
    return jax.shard_map(
        functools.partial(shards, slabs, mems),
        mesh=mesh,
        in_specs=(
            P("mem", None, "slab", None),
            P("mem", None, None, "slab", None),
            P("slab", None),
            P(None, "slab", None),
            P(),
            P(),
            P(),
            P(),
            P(),
            P(),
        ),
        out_specs=P("mem", None, None, "slab", None),
        check_vma=False,
    )
```

```python
import functools

import jax
import jax.numpy as jnp
from jax import lax
from jax.experimental import pallas as pl
from jax.experimental.pallas import tpu as pltpu
from jax.sharding import PartitionSpec as P

NY = 4
NC = 2
HIGHEST = lax.Precision.HIGHEST
F32 = jnp.float32
MESH = pl.DeviceIdType.MESH


def sides(x):
    rows = x.shape[0]
    row = lax.broadcasted_iota(jnp.int32, x.shape, 0) % 4
    lane = lax.broadcasted_iota(jnp.int32, x.shape, 1)
    left = pltpu.roll(x, 1, 1)
    right = pltpu.roll(x, 127, 1)
    before = jnp.where(row == 0, 0.0, pltpu.roll(left, 1, 0))
    after = jnp.where(row == 3, 0.0, pltpu.roll(right, rows - 1, 0))
    return jnp.where(lane == 0, before, left), jnp.where(lane == 127, after, right)


def gather_kernel(
    slabs,
    mems,
    cur_ref,
    delayed_ref,
    spread_ref,
    ratio_ref,
    row_ref,
    col_ref,
    field_ref,
    obs_ref,
    state_ref,
    above_ref,
    below_ref,
    fore_ref,
    smooth_ref,
    part_ref,
    ybuf,
    ysum,
    zbuf,
    zsum,
    hot_ref,
    send_sem,
    recv_sem,
    local_sem,
):
    nz, nx = slabs // NY, mems // NC
    slab, mem = lax.axis_index("slab"), lax.axis_index("mem")
    z, y = slab // NY, slab % NY
    xc, core = mem // NC, mem % NC
    members, depth = cur_ref.shape[0], cur_ref.shape[1]
    rows = members * depth

    nxt = (lax.rem(slab + 1, slabs), mem)
    prv = (lax.rem(slab + slabs - 1, slabs), mem)
    ypeer = [(z * NY + lax.rem(y + d, NY), mem) for d in range(NY)]
    zpeer = [(lax.rem(z + d, nz) * NY + y, mem) for d in range(nz)]
    plane = [
        (z * NY + lax.rem(y + dy, NY), lax.rem(mem + dm, mems))
        for dm in range(mems)
        for dy in range(NY)
    ][1:]
    xpeer = [(slab, lax.rem(xc + d, nx) * NC + core) for d in range(nx)]
    twin = (slab, xc * NC + (1 - core))

    barrier = pltpu.get_barrier_semaphore()
    greeted = [nxt, prv] + zpeer[1:] + plane
    for peer in greeted:
        pl.semaphore_signal(barrier, inc=1, device_id=peer, device_id_type=MESH)
    cur = cur_ref[...].reshape(rows, 128)
    left, right = sides(cur)

    def every(c):
        block = jnp.concatenate([c] * (depth // 4), axis=0)
        return jnp.broadcast_to(block[None], (members, depth, 128)).reshape(rows, 128)

    spread = every(spread_ref[...])
    ratio0 = every(ratio_ref[0])
    ratio1 = every(ratio_ref[1])
    inner = cur + spread * (right + left - 4.0 * cur) - ratio1 * (right - left) * 0.5
    fore_ref[...] = inner.reshape(members, depth, 128)
    from_below = spread - 0.5 * ratio0
    from_above = spread + 0.5 * ratio0
    place = jnp.where(row_ref[...] == slab, field_ref[...] * 512 + col_ref[...], -1)
    place = jnp.concatenate([place[b : b + 1] for b in range(place.shape[0])], axis=1)
    total = place.shape[1]
    spot = lax.broadcasted_iota(jnp.int32, (256, total), 0)
    for g in range(depth // 2):
        hot_ref[g] = jnp.where(spot + 256 * g == place, 1.0, 0.0).astype(jnp.bfloat16)
    pl.semaphore_wait(barrier, len(greeted))

    used = [0]

    def send(src, dst, peer):
        k = used[0]
        used[0] += 1
        copy = pltpu.make_async_remote_copy(
            src_ref=src,
            dst_ref=dst,
            send_sem=send_sem.at[k],
            recv_sem=recv_sem.at[k],
            device_id=peer,
            device_id_type=MESH,
        )
        copy.start()
        return copy

    halo = [send(cur_ref, above_ref, nxt), send(cur_ref, below_ref, prv)]
    lagged = pl.ds(depth, delayed_ref.shape[1])
    level0 = pl.ds(0, depth)
    bulk = [send(delayed_ref, state_ref.at[mem, :, lagged, :], xpeer[d]) for d in range(1, nx)]
    keep = pltpu.make_async_copy(delayed_ref, state_ref.at[mem, :, lagged, :], local_sem.at[0])
    keep.start()

    for copy in halo:
        copy.wait_recv()
    above = jnp.where(slab > 0, above_ref[...].reshape(rows, 128), 0.0)
    below = jnp.where(slab < slabs - 1, below_ref[...].reshape(rows, 128), 0.0)
    inner = fore_ref[...].reshape(rows, 128)
    forecast = inner + from_below * below + from_above * above
    fore_ref[...] = forecast.reshape(members, depth, 128)
    for d in range(1, nx):
        bulk.append(send(fore_ref, state_ref.at[mem, :, level0, :], xpeer[d]))
    keep0 = pltpu.make_async_copy(fore_ref, state_ref.at[mem, :, level0, :], local_sem.at[1])
    keep0.start()

    left, right = sides(forecast)
    smooth = 0.25 * left + 0.5 * forecast + 0.25 * right
    smooth_ref[...] = smooth.reshape(members, depth, 128)
    acc = jnp.zeros((3 * members, total), F32)
    for g in range(depth // 2):
        values = jnp.concatenate([smooth_ref[:, 2 * g, :], smooth_ref[:, 2 * g + 1, :]], axis=1)
        high = values.astype(jnp.bfloat16).astype(F32)
        rest = values - high
        middle = rest.astype(jnp.bfloat16).astype(F32)
        low = rest - middle
        lhs = jnp.concatenate([high, middle, low], axis=0).astype(jnp.bfloat16)
        acc = acc + jnp.dot(lhs, hot_ref[g], preferred_element_type=F32)
    picked = acc[:members] + acc[members : 2 * members] + acc[2 * members :]
    for q in range(NY):
        part_ref[q] = picked[:, q * 128 : (q + 1) * 128]

    ysend = [send(part_ref.at[lax.rem(y + d, NY)], ybuf.at[d], ypeer[d]) for d in range(1, NY)]
    value = part_ref[y]
    for d, copy in enumerate(ysend, 1):
        copy.wait_recv()
        value = value + ybuf[d]
    ysum[...] = value

    far = sorted(range(1, nz), key=lambda d: -min(d, nz - d))
    zsend = [send(ysum, zbuf.at[d], zpeer[d]) for d in far]
    keep.wait()
    keep0.wait()
    for copy in bulk:
        copy.wait_recv()
    forward = []
    for d in range(nx):
        block = state_ref.at[lax.rem(xc + d, nx) * NC + core]
        forward.append(send(block, block, twin))

    for d, copy in reversed(list(zip(far, zsend))):
        copy.wait_recv()
        value = value + zbuf[d]
    zsum[...] = value
    obs_ref[mem, y] = value
    tiles = [send(zsum, obs_ref.at[mem, y], peer) for peer in plane]
    for copy in tiles:
        copy.wait_recv()
    for copy in forward:
        copy.wait_recv()
    for copy in halo + bulk + ysend + zsend + forward + tiles:
        copy.wait_send()


def eliminate(system, n):
    row = lax.broadcasted_iota(jnp.int32, system.shape, 0)
    panel = 16
    for base in range(0, n, panel):
        columns = [
            jnp.broadcast_to(system[:, n + base + i : n + base + i + 1], system.shape)
            for i in range(panel)
        ]
        for i in range(panel):
            k = base + i
            mine = row == k
            column = columns[i]
            inverse = 1.0 / column[k : k + 1, :]
            pivot = system[k : k + 1, :] * inverse
            system = jnp.where(mine, pivot, system - column * pivot)
            for j in range(i + 1, panel):
                scale = columns[j][k : k + 1, :] * inverse
                columns[j] = jnp.where(mine, scale, columns[j] - column * scale)
    return system[:, :n]


def split(x):
    high = x.astype(jnp.bfloat16)
    return high, (x - high.astype(F32)).astype(jnp.bfloat16)


def update_kernel(value_ref, error_ref, noise_ref, obs_ref, state_hbm, out_ref, matrix_ref, state_ref, load_sem):
    load = pltpu.make_async_copy(state_hbm, state_ref, load_sem)
    load.start()
    mems, pieces, members, width = obs_ref.shape
    n = mems * members
    batches = value_ref.shape[0]
    per = pieces // batches
    eye = jnp.where(
        lax.broadcasted_iota(jnp.int32, (n, n), 0) == lax.broadcasted_iota(jnp.int32, (n, n), 1),
        1.0,
        0.0,
    )
    shifted = jnp.where(
        lax.broadcasted_iota(jnp.int32, (n, 2 * n), 0) + n
        == lax.broadcasted_iota(jnp.int32, (n, 2 * n), 1),
        n - 1.0,
        0.0,
    )
    so_far = None
    for b in range(batches):
        observed = jnp.concatenate(
            [obs_ref[:, q].reshape(n, width) for q in range(b * per, (b + 1) * per)], axis=1
        )
        if so_far is not None:
            observed = jnp.dot(so_far, observed, precision=HIGHEST, preferred_element_type=F32)
        error = error_ref[b : b + 1, :]
        scaled = (observed - jnp.mean(observed, axis=0, keepdims=True)) / error
        innovation = (value_ref[b : b + 1, :] - observed) / error + noise_ref[b]
        both = jnp.concatenate([innovation, scaled], axis=0)
        system = shifted + lax.dot_general(
            scaled, both, (((1,), (1,)), ((), ())), precision=HIGHEST, preferred_element_type=F32
        )
        weights = eliminate(system, n)
        matrix = (eye + weights - jnp.mean(weights, axis=0, keepdims=True)).T
        if so_far is None:
            so_far = matrix
        else:
            so_far = jnp.dot(matrix, so_far, precision=HIGHEST, preferred_element_type=F32)
    matrix_ref[...] = so_far
    start = pl.multiple_of(lax.axis_index("mem") * members, members)
    mine = matrix_ref[pl.ds(start, members), :]
    high, low = split(mine)
    lhs = jnp.concatenate([high.astype(F32), low.astype(F32), high.astype(F32)], axis=1)
    lhs = lhs.astype(jnp.bfloat16)
    load.wait()
    for t in range(0, state_ref.shape[2], 2):
        block = jnp.concatenate(
            [state_ref[:, :, t + i, :].reshape(n, 128) for i in range(2)], axis=1
        )
        high, low = split(block)
        rhs = jnp.concatenate([high, high, low], axis=0)
        result = jnp.dot(lhs, rhs, preferred_element_type=F32)
        for i in range(2):
            out_ref[:, t + i, :] = result[:, i * 128 : (i + 1) * 128]


def shards(
    slabs,
    mems,
    present_ensemble,
    delayed_ensemble,
    spreading_coefficient,
    transport_ratios,
    obs_value,
    obs_error,
    obs_noise,
    obs_row,
    obs_col,
    obs_field,
):
    members, fields = present_ensemble.shape[:2]
    lags = delayed_ensemble.shape[1]
    depth = fields * 4
    levels = (lags + 1) * depth
    nx = mems // NC
    copies = 2 + 2 * (nx - 1) + (NY - 1) + (slabs // NY - 1) + (NY * mems - 1) + nx
    vmem = pl.BlockSpec(memory_space=pltpu.VMEM)
    observed, state = pl.pallas_call(
        functools.partial(gather_kernel, slabs, mems),
        out_shape=(
            jax.ShapeDtypeStruct((mems, NY, members, 128), F32),
            jax.ShapeDtypeStruct((mems, members, levels, 128), F32),
        ),
        in_specs=[vmem] * 7,
        out_specs=(vmem, pl.BlockSpec(memory_space=pl.ANY)),
        scratch_shapes=[
            pltpu.VMEM((members, depth, 128), F32),
            pltpu.VMEM((members, depth, 128), F32),
            pltpu.VMEM((members, depth, 128), F32),
            pltpu.VMEM((members, depth, 128), F32),
            pltpu.VMEM((NY, members, 128), F32),
            pltpu.VMEM((NY, members, 128), F32),
            pltpu.VMEM((members, 128), F32),
            pltpu.VMEM((slabs // NY, members, 128), F32),
            pltpu.VMEM((members, 128), F32),
            pltpu.VMEM((depth // 2, 256, obs_row.size), jnp.bfloat16),
            pltpu.SemaphoreType.DMA((copies,)),
            pltpu.SemaphoreType.DMA((copies,)),
            pltpu.SemaphoreType.DMA((2,)),
        ],
        compiler_params=pltpu.CompilerParams(collective_id=0, has_side_effects=True),
        name="gather",
    )(
        present_ensemble.reshape(members, depth, 128),
        delayed_ensemble.reshape(members, lags * depth, 128),
        spreading_coefficient.reshape(4, 128),
        transport_ratios.reshape(2, 4, 128),
        obs_row,
        obs_col,
        obs_field,
    )
    result = pl.pallas_call(
        update_kernel,
        out_shape=jax.ShapeDtypeStruct((members, levels, 128), F32),
        in_specs=[vmem] * 4 + [pl.BlockSpec(memory_space=pl.ANY)],
        out_specs=vmem,
        scratch_shapes=[
            pltpu.VMEM((mems * members, mems * members), F32),
            pltpu.VMEM((mems, members, levels, 128), F32),
            pltpu.SemaphoreType.DMA,
        ],
        name="update",
    )(obs_value, obs_error, obs_noise, observed, state)
    return result.reshape(members, lags + 1, fields, 1, 512)


def solution(mesh):
    slabs, mems = mesh.shape["slab"], mesh.shape["mem"]
    return jax.shard_map(
        functools.partial(shards, slabs, mems),
        mesh=mesh,
        in_specs=(
            P("mem", None, "slab", None),
            P("mem", None, None, "slab", None),
            P("slab", None),
            P(None, "slab", None),
            P(),
            P(),
            P(),
            P(),
            P(),
            P(),
        ),
        out_specs=P("mem", None, None, "slab", None),
        check_vma=False,
    )
```
